32 devices in a mesh: gx: 4 (over z), gy: 2 (over x), gz: 4 (over y, core).
Axes of the slice: x: 2, y: 2, z: 4, core: 2. Of those that a mesh axis runs over, the one named last changes fastest.
Arguments:
- orbitals: bfloat16 [8, 128, 8192], P(None, 'gx', ('gy', 'gz')), may hold values from -6 to 6
- potential: float32 [64, 32, 64], P('gx', 'gy', 'gz'), may hold values from -3 to 0
- ion_potential: float32 [64, 32, 64], P('gx', 'gy', 'gz'), may hold values from -2 to 0
- occupations: float32 [8], replicated, may hold values from 0.005 to 0.08
Outputs:
- new_orbitals: bfloat16 [8, 128, 8192], P(None, 'gx', ('gy', 'gz'))
- density: float32 [64, 32, 64], P('gx', 'gy', 'gz')
- new_potential: float32 [128, 8192], P('gx', ('gy', 'gz'))
The draws below stay inside these ranges and needn't reach their ends.
All inputs are finite; a program needn't handle non-finite values.
Results may differ from the reference program's by a relative error of at most 0.001.
Values sent between devices are 32-bit elements; how exact they have to be, the bound alone decides.
A program may use at most 64 MiB of HBM per device.

```python
import math
import jax
import jax.numpy as jnp
from jax import lax

CORE = 16
BUF = 8
NORB = 8
DEGREE = 10
LX = 32
NX = 64
NY = 32
NZ = 64
N_GX = 4
N_GY = 2
N_GZ = 4


def steps_of(rng, dims, shards, least, largest):
    def one(dim, blocks):
        heights = jax.random.uniform(jax.random.fold_in(jax.random.fold_in(rng, 6), dim), (blocks,), jnp.float32, least / len(shards), largest / len(shards))
        return jnp.repeat(jnp.exp(heights), dims[dim] // blocks).reshape((-1,) + (1,) * (len(dims) - dim - 1))

    level = one(*shards[0])
    for cut in shards[1:]:
        level = level * one(*cut)
    return level


def bell_draw(key, shape, deviation, limit, cuts=(), kind=jnp.bfloat16):
    values = jax.random.normal(key, shape, jnp.float32) * deviation
    if len(cuts) > 0:
        values = steps_of(key, shape, cuts, -0.22, 0.18) * values
    return jnp.clip(values, min=-limit, max=limit).astype(kind)


def setup_inputs(seed: int = 0) -> dict:
    streams_of = jax.random.split(jax.random.key(seed), 5)
    return {
        "orbitals": bell_draw(streams_of[0], (NORB, N_GX * LX, N_GY * N_GZ * LX * LX), 1.0, 6.0, ((1, 4), (2, 8))),
        "potential": jnp.clip(-3.0 + 3.0 * jax.random.uniform(streams_of[1], (NX, NY, NZ), jnp.float32) ** steps_of(streams_of[1], (NX, NY, NZ), ((0, 4), (1, 2), (2, 4)), -0.2, 0.2), -3.0, 0.0),
        "ion_potential": jnp.clip(-2.0 + 2.0 * jax.random.uniform(streams_of[2], (NX, NY, NZ), jnp.float32) ** steps_of(streams_of[2], (NX, NY, NZ), ((0, 4), (1, 2), (2, 4)), -0.2, 0.2), -2.0, 0.0),
        "occupations": jnp.clip(jnp.exp(jax.random.uniform(streams_of[3], (NORB,), jnp.float32, math.log(0.005), math.log(0.08))), 0.005, 0.08),
    }


spacing = 0.2
kinetic = 0.5 / (spacing * spacing)
filter_low = 6.0
filter_high = 12.0 * kinetic
centre_value = 0.5 * (filter_low + filter_high)
half_width = 0.5 * (filter_high - filter_low)

def hamiltonian(vectors, potential_ext, edge_len):
    extent = vectors.shape[2]
    padded = jnp.pad(vectors, ((0, 0), (1, 1), (0, 0)))
    beside = padded[:, 2:] + padded[:, :-2]
    padded = jnp.pad(vectors, ((0, 0), (0, 0), (edge_len, edge_len)))
    beside = beside + padded[:, :, 2 * edge_len:] + padded[:, :, :-2 * edge_len]
    padded = jnp.pad(vectors, ((0, 0), (0, 0), (1, 1)))
    column = jnp.arange(extent, dtype=jnp.int32) % edge_len
    up_mask = (column < edge_len - 1).astype(vectors.dtype)
    down_mask = (column > 0).astype(vectors.dtype)
    beside = beside + padded[:, :, 2:] * up_mask + padded[:, :, :-2] * down_mask
    return -kinetic * (beside - 6.0 * vectors) + potential_ext * vectors

def chebyshev(initial, potential_ext, edge_len):
    leading = (hamiltonian(initial, potential_ext, edge_len) - centre_value * initial) / half_width

    def advance(counter, states):
        previous, current = states
        following = 2.0 * (hamiltonian(current, potential_ext, edge_len) - centre_value * current) / half_width - previous
        return (current, following)
    return lax.fori_loop(1, DEGREE, advance, (initial, leading))[1]

def orthonormal(filtered):
    orbital_count = filtered.shape[0]
    flattened = filtered.reshape(orbital_count, -1)
    intersection = jnp.dot(flattened, flattened.T, precision=lax.Precision.HIGHEST) / flattened.shape[1]
    factor = jnp.linalg.cholesky(intersection)
    identity = jnp.eye(orbital_count, dtype=filtered.dtype)
    inverse = lax.linalg.triangular_solve(factor, identity, left_side=True, lower=True)
    return jnp.dot(inverse, flattened, precision=lax.Precision.HIGHEST).reshape(filtered.shape)

def ramp(extent):
    position = jnp.arange(extent, dtype=jnp.float32)
    rising = jnp.clip((position + 0.5 - 0.5 * BUF) / BUF, 0.0, 1.0)
    falling = jnp.clip((extent - 0.5 * BUF - 0.5 - position) / BUF, 0.0, 1.0)
    return rising * falling

def window_weight(edge_len):
    profile = ramp(edge_len)
    return profile[:, None] * (profile[:, None] * profile[None, :]).reshape(1, edge_len * edge_len)

def exchange_correlation(density):
    cube_root = jnp.cbrt(density)
    slater = -(3.0 / math.pi) ** (1.0 / 3.0) * cube_root
    radius = (3.0 / (4.0 * math.pi)) ** (1.0 / 3.0)
    bottom = radius + 7.8 * cube_root
    wigner = -0.44 * cube_root / bottom * (1.0 + radius / (3.0 * bottom))
    return slater + wigner

def wave_term(extent, initial, period):
    indices = (initial + jnp.arange(extent, dtype=jnp.int32)).astype(jnp.float32)
    return 4.0 / (spacing * spacing) * jnp.sin(math.pi * indices / period) ** 2

def kernel(extents, starts, periods):
    eigen_sum = wave_term(extents[0], starts[0], periods[0])[:, None, None] + wave_term(extents[1], starts[1], periods[1])[None, :, None] + wave_term(extents[2], starts[2], periods[2])[None, None, :]
    positive = eigen_sum > 0.0
    return jnp.where(positive, 4.0 * math.pi / jnp.where(positive, eigen_sum, 1.0), 0.0)

def offsets(count):
    return jnp.arange(count, dtype=jnp.int32)[:, None] * CORE + jnp.arange(LX, dtype=jnp.int32)[None, :]

def windows(field):
    padded = jnp.pad(field, BUF, mode='wrap')
    picked = jnp.take(padded, offsets(N_GX), axis=0)
    picked = jnp.take(picked, offsets(N_GY), axis=2)
    return jnp.take(picked, offsets(N_GZ), axis=4)

def fold_axis(values, dom_axis, loc_axis):
    low_rows = lax.slice_in_dim(values, 0, BUF, axis=loc_axis)
    interior = lax.slice_in_dim(values, BUF, BUF + CORE, axis=loc_axis)
    high_rows = lax.slice_in_dim(values, BUF + CORE, LX, axis=loc_axis)
    pad_low = [(0, 0)] * values.ndim
    pad_low[loc_axis] = (CORE - BUF, 0)
    pad_high = [(0, 0)] * values.ndim
    pad_high[loc_axis] = (0, CORE - BUF)
    return interior + jnp.pad(jnp.roll(low_rows, -1, axis=dom_axis), pad_low) + jnp.pad(jnp.roll(high_rows, 1, axis=dom_axis), pad_high)

def reference(orbitals, potential, ion_potential, occupations):
    domains = N_GX * N_GY * N_GZ
    plane_cells = LX * LX
    stacked = orbitals.reshape(NORB, N_GX, LX, N_GY * N_GZ, plane_cells).transpose(1, 3, 0, 2, 4)
    stacked = stacked.reshape(domains, NORB, LX, plane_cells)
    fields = windows(potential).transpose(0, 2, 4, 1, 3, 5).reshape(domains, LX, plane_cells)
    weight = window_weight(LX)

    def domain_work(states):
        initial, potential_ext = states
        filtered = chebyshev(initial.astype(jnp.float32), potential_ext, LX)
        normal_set = orthonormal(filtered)
        partial_value = weight * jnp.sum(occupations[:, None, None] * normal_set * normal_set, axis=0)
        return (normal_set.astype(jnp.bfloat16), partial_value)
    new_stack, partials = lax.map(domain_work, (stacked, fields))
    new_orbitals = new_stack.reshape(N_GX, N_GY * N_GZ, NORB, LX, plane_cells).transpose(2, 0, 3, 1, 4)
    new_orbitals = new_orbitals.reshape(NORB, N_GX * LX, N_GY * N_GZ * plane_cells)
    values = partials.reshape(N_GX, N_GY, N_GZ, LX, LX, LX)
    values = fold_axis(values, 0, 3)
    values = fold_axis(values, 1, 4)
    values = fold_axis(values, 2, 5)
    density = values.transpose(0, 3, 1, 4, 2, 5).reshape(NX, NY, NZ)
    kernel_grid = kernel((NX, NY, NZ), (0, 0, 0), (NX, NY, NZ))
    hartree = jnp.real(jnp.fft.ifftn(jnp.fft.fftn(density) * kernel_grid)).astype(density.dtype)
    interior = ion_potential + hartree + exchange_correlation(density)
    new_potential = windows(interior).transpose(0, 1, 2, 4, 3, 5).reshape(N_GX * LX, N_GY * N_GZ * plane_cells)
    return (new_orbitals, density, new_potential)
```

```python
import functools
import math

import jax
import jax.numpy as jnp
import numpy as np
from jax import lax
from jax.experimental import pallas as pl
from jax.experimental.pallas import tpu as pltpu
from jax.sharding import PartitionSpec as P

BUF = 8
DEGREE = 10
MESH = pl.DeviceIdType.MESH

spacing = 0.2
kinetic = 0.5 / (spacing * spacing)
filter_low = 6.0
filter_high = 12.0 * kinetic
centre_value = 0.5 * (filter_low + filter_high)
half_width = 0.5 * (filter_high - filter_low)

OFFSETS = [
    (dx, dy, dz)
    for dz in (-1, 0, 1)
    for dx in (-1, 0, 1)
    for dy in (-1, 0, 1)
    if (dx, dy, dz) != (0, 0, 0)
]


def here():
    return lax.axis_index("gx"), lax.axis_index("gy"), lax.axis_index("gz")


def moved(place, offset, counts):
    return tuple(lax.rem(p + (o % n), n) for p, o, n in zip(place, offset, counts))


def distinct(offsets, counts):
    found = []
    for offset in offsets:
        wrapped = tuple(o % n for o, n in zip(offset, counts))
        if any(wrapped) and wrapped not in found:
            found.append(wrapped)
    return found


def greet(offsets, counts):
    barrier = pltpu.get_barrier_semaphore()
    place = here()
    others = distinct(offsets, counts)
    if len(others) <= 64:
        for offset in others:
            pl.semaphore_signal(
                barrier, inc=1, device_id=moved(place, offset, counts), device_id_type=MESH
            )
    else:
        total = counts[0] * counts[1] * counts[2]

        def signal(index, carry):
            offset = (
                index // (counts[1] * counts[2]),
                (index // counts[2]) % counts[1],
                index % counts[2],
            )
            target = tuple(lax.rem(p + o, n) for p, o, n in zip(place, offset, counts))
            pl.semaphore_signal(barrier, inc=1, device_id=target, device_id_type=MESH)
            return carry

        lax.fori_loop(1, total, signal, 0)
    pl.semaphore_wait(barrier, len(others))


def lanes(shape):
    return lax.broadcasted_iota(jnp.int32, shape, len(shape) - 1)


ROWS = {-1: (8, 8, 0), 0: (0, 16, 8), 1: (0, 8, 24)}
CHUNKS = {-1: (2, 2, 0), 0: (0, 4, 2), 1: (0, 2, 6)}


def halo_kernel(counts, fields_ref, out_ref, block, send_sem, recv_sem):
    place = here()
    greet(OFFSETS, counts)
    for field in range(2):
        for chunk in range(4):
            total = None
            for inner in range(4):
                piece = fields_ref[field, :, 4 * chunk + inner, :]
                piece = pltpu.roll(piece, 32 * inner + 8, 1)
                total = piece if total is None else total + piece
            block[field, chunk] = total
    out_ref[1, :, 2:6, 8:24, :] = block[...]
    copies = []
    for number, (dx, dy, dz) in enumerate(OFFSETS):
        row, rows, to_row = ROWS[dx]
        chunk, chunks, to_chunk = CHUNKS[dy]
        copy = pltpu.make_async_remote_copy(
            src_ref=block.at[:, pl.ds(chunk, chunks), pl.ds(row, rows), :],
            dst_ref=out_ref.at[dz + 1, :, pl.ds(to_chunk, chunks), pl.ds(to_row, rows), :],
            send_sem=send_sem.at[number],
            recv_sem=recv_sem.at[number],
            device_id=moved(place, (-dx, -dy, -dz), counts),
            device_id_type=MESH,
        )
        copy.start()
        copies.append(copy)
    for copy in copies:
        copy.wait()


def halo(fields, counts):
    return pl.pallas_call(
        functools.partial(halo_kernel, counts),
        out_shape=jax.ShapeDtypeStruct((3, 2, 8, 32, 128), jnp.float32),
        in_specs=[pl.BlockSpec(memory_space=pltpu.VMEM)],
        out_specs=pl.BlockSpec(memory_space=pltpu.VMEM),
        scratch_shapes=[
            pltpu.VMEM((2, 4, 16, 128), jnp.float32),
            pltpu.SemaphoreType.DMA((len(OFFSETS),)),
            pltpu.SemaphoreType.DMA((len(OFFSETS),)),
        ],
        compiler_params=pltpu.CompilerParams(collective_id=0, has_side_effects=True),
        name="halo",
    )(fields)


def joined(below, own, above):
    cell = lanes(own.shape) % 32
    below = pltpu.roll(below, 112, own.ndim - 1)
    above = pltpu.roll(above, 16, own.ndim - 1)
    return jnp.where(cell < 8, below, jnp.where(cell < 24, own, above))


def ramp(position):
    rising = jnp.clip((position + 0.5 - 0.5 * BUF) / BUF, 0.0, 1.0)
    falling = jnp.clip((32 - 0.5 * BUF - 0.5 - position) / BUF, 0.0, 1.0)
    return rising * falling


def filter_kernel(occ_ref, orbitals_ref, halo_ref, new_ref, part_ref, first, second, diag):
    norb = orbitals_ref.shape[0]
    lane = lanes((32, 128))
    cell = lane % 32
    not_last = cell < 31
    not_first = cell > 0
    inner_up = lane < 96
    inner_down = lane >= 32
    side = kinetic * 2.0 / half_width

    edge = jnp.zeros((8, 128), jnp.float32)

    def prepare(chunk, carry):
        field = joined(halo_ref[0, 0, chunk], halo_ref[1, 0, chunk], halo_ref[2, 0, chunk])
        diag[chunk] = (field + (6.0 * kinetic - centre_value)) * (2.0 / half_width)
        return carry

    lax.fori_loop(0, 8, prepare, 0)

    def fill(orbital, carry):
        for chunk in range(8):
            first[orbital, chunk, 8:40, :] = orbitals_ref[
                orbital, :, 128 * chunk : 128 * chunk + 128
            ].astype(jnp.float32)
            for ref in (first, second):
                ref[orbital, chunk, 0:8, :] = edge
                ref[orbital, chunk, 40:48, :] = edge
        return carry

    lax.fori_loop(0, norb, fill, 0)

    def step(source, target, start):
        def one(orbital, carry):
            values = [source[orbital, chunk, 8:40, :] for chunk in range(8)]
            ups = [pltpu.roll(v, 96, 1) for v in values]
            downs = [pltpu.roll(v, 32, 1) for v in values]
            for chunk in range(8):
                value = values[chunk]
                beside = source[orbital, chunk, 7:39, :] + source[orbital, chunk, 9:41, :]
                after = ups[chunk + 1] if chunk < 7 else 0.0
                before = downs[chunk - 1] if chunk > 0 else 0.0
                beside = beside + jnp.where(inner_up, ups[chunk], after)
                beside = beside + jnp.where(inner_down, downs[chunk], before)
                beside = beside + jnp.where(not_last, pltpu.roll(value, 127, 1), 0.0)
                beside = beside + jnp.where(not_first, pltpu.roll(value, 1, 1), 0.0)
                result = diag[chunk] * value - side * beside
                if start:
                    result = 0.5 * result
                else:
                    result = result - target[orbital, chunk, 8:40, :]
                target[orbital, chunk, 8:40, :] = result
            return carry

        lax.fori_loop(0, norb, one, 0)

    step(first, second, True)

    def pair(counter, carry):
        step(second, first, False)
        step(first, second, False)
        return carry

    lax.fori_loop(0, (DEGREE - 1) // 2, pair, 0)
    step(second, first, False)
    filtered = first

    pairs = [(i, j) for i in range(norb) for j in range(i + 1)]

    def gram(index, sums):
        chunk = index // 4
        row = pl.multiple_of(8 + 8 * (index % 4), 8)
        vectors = [filtered[n, chunk, pl.ds(row, 8), :] for n in range(norb)]
        return tuple(s + vectors[i] * vectors[j] for s, (i, j) in zip(sums, pairs))

    zero = jnp.zeros((8, 128), jnp.float32)
    sums = lax.fori_loop(0, 32, gram, (zero,) * len(pairs))
    scale = 1.0 / 32768.0
    matrix = {}
    for key, total in zip(pairs, sums):
        total = jnp.sum(jnp.sum(total, axis=0, keepdims=True), axis=1, keepdims=True)
        matrix[key] = jnp.broadcast_to(total * scale, (8, 128))
    factor = {}
    inverse = {}
    for j in range(norb):
        recip = 1.0 / jnp.sqrt(matrix[(j, j)])
        inverse[(j, j)] = recip
        for i in range(j + 1, norb):
            factor[(i, j)] = matrix[(i, j)] * recip
        for i in range(j + 1, norb):
            for k in range(j + 1, i + 1):
                matrix[(i, k)] = matrix[(i, k)] - factor[(i, j)] * factor[(k, j)]
    for i in range(norb):
        for j in range(i):
            total = None
            for k in range(j, i):
                term = factor[(i, k)] * inverse[(k, j)]
                total = term if total is None else total + term
            inverse[(i, j)] = -total * inverse[(i, i)]
    occ = [jnp.full((8, 128), occ_ref[n], jnp.float32) for n in range(norb)]

    lane8 = lanes((8, 128))
    along_c = ramp((lane8 % 32).astype(jnp.float32))
    row8 = lax.broadcasted_iota(jnp.int32, (8, 128), 0)

    def finish(index, carry):
        half = index % 2
        for chunk in (index // 2,):
            along_b = ramp((4 * chunk + lane8 // 32).astype(jnp.float32))
            plane = along_b * along_c
            halves = []
            for tile in range(2):
                row = pl.multiple_of(8 + 16 * half + 8 * tile, 8)
                vectors = [filtered[n, chunk, pl.ds(row, 8), :] for n in range(norb)]
                density = None
                results = []
                for i in range(norb):
                    total = inverse[(i, 0)] * vectors[0]
                    for j in range(1, i + 1):
                        total = total + inverse[(i, j)] * vectors[j]
                    results.append(total)
                    term = occ[i] * total * total
                    density = term if density is None else density + term
                along_a = ramp((16 * half + 8 * tile + row8).astype(jnp.float32))
                part_ref[chunk, pl.ds(pl.multiple_of(16 * half + 8 * tile, 8), 8), :] = (
                    along_a * plane * density
                )
                halves.append(results)
            column = pl.multiple_of(128 * chunk, 128)
            for i in range(norb):
                both = jnp.concatenate([halves[0][i], halves[1][i]], axis=0)
                new_ref[i, pl.ds(pl.multiple_of(16 * half, 16), 16), pl.ds(column, 128)] = (
                    both.astype(jnp.bfloat16)
                )
        return carry

    lax.fori_loop(0, 16, finish, 0)


def filter_orbitals(occupations, orbitals, windows):
    norb = orbitals.shape[0]
    return pl.pallas_call(
        filter_kernel,
        out_shape=(
            jax.ShapeDtypeStruct(orbitals.shape, jnp.bfloat16),
            jax.ShapeDtypeStruct((8, 32, 128), jnp.float32),
        ),
        in_specs=[
            pl.BlockSpec(memory_space=pltpu.SMEM),
            pl.BlockSpec(memory_space=pltpu.VMEM),
            pl.BlockSpec(memory_space=pltpu.VMEM),
        ],
        out_specs=(
            pl.BlockSpec(memory_space=pltpu.VMEM),
            pl.BlockSpec(memory_space=pltpu.VMEM),
        ),
        scratch_shapes=[
            pltpu.VMEM((norb, 8, 48, 128), jnp.float32),
            pltpu.VMEM((norb, 8, 48, 128), jnp.float32),
            pltpu.VMEM((8, 32, 128), jnp.float32),
        ],
        name="filter",
    )(occupations, orbitals, windows)


FOLD_ROWS = {-1: (0, 8, 8), 0: (8, 16, 0), 1: (24, 8, 0)}
FOLD_CHUNKS = {-1: (1, 1, 3), 0: (2, 4, 0), 1: (6, 1, 0)}


def gather_kernel(counts, part_ref, all_ref, inbox, block, send_sem, recv_sem, hop_send, hop_recv,
                  pass_send, pass_recv):
    nx, ny, nz = counts
    place = here()
    everyone = [(x, y, z) for x in range(nx) for y in range(ny) for z in range(nz)]
    greet(everyone, counts)
    copies = []
    for number, (dx, dy, dz) in enumerate(OFFSETS):
        row, rows, _ = FOLD_ROWS[dx]
        chunk, chunks, _ = FOLD_CHUNKS[dy]
        copy = pltpu.make_async_remote_copy(
            src_ref=part_ref.at[pl.ds(chunk, chunks), pl.ds(row, rows), :],
            dst_ref=inbox.at[number, pl.ds(0, chunks), pl.ds(0, rows), :],
            send_sem=send_sem.at[number],
            recv_sem=recv_sem.at[number],
            device_id=moved(place, (dx, dy, dz), counts),
            device_id_type=MESH,
        )
        copy.start()
        copies.append(copy)
    for copy in copies:
        copy.wait()
    cell = lanes((16, 128)) % 32
    sums = {}
    for chunk in range(4):
        for dz in (-1, 0, 1):
            low = part_ref[2 + chunk, 8:16, :] if dz == 0 else jnp.zeros((8, 128), jnp.float32)
            high = part_ref[2 + chunk, 16:24, :] if dz == 0 else jnp.zeros((8, 128), jnp.float32)
            for number, (dx, dy, other) in enumerate(OFFSETS):
                if other != dz:
                    continue
                _, chunks, to_chunk = FOLD_CHUNKS[dy]
                if not to_chunk <= chunk < to_chunk + chunks:
                    continue
                at = chunk - to_chunk
                if dx == 0:
                    low = low + inbox[number, at, 0:8, :]
                    high = high + inbox[number, at, 8:16, :]
                elif dx == 1:
                    low = low + inbox[number, at, 0:8, :]
                else:
                    high = high + inbox[number, at, 0:8, :]
            total = jnp.concatenate([low, high], axis=0)
            if dz == 1:
                total = jnp.where((cell >= 8) & (cell < 12), pltpu.roll(total, 112, 1), 0.0)
            elif dz == -1:
                total = jnp.where((cell >= 20) & (cell < 24), pltpu.roll(total, 16, 1), 0.0)
            sums[chunk] = total if dz == -1 else sums[chunk] + total
    for part in range(2):
        merged = jnp.where(
            cell < 16, pltpu.roll(sums[2 * part], 120, 1), pltpu.roll(sums[2 * part + 1], 8, 1)
        )
        block[part] = merged
        all_ref[0, part, 0, 0:16, :] = merged

    parity = lax.rem(place[2], 2)
    partner = (place[0], place[1], place[2] + 1 - 2 * parity)
    pairs = nz // 2
    chips = nx * ny * pairs

    def split(index):
        return index // (ny * pairs), (index // pairs) % ny, 2 * (index % pairs)

    def hop(index):
        ox, oy, oz = split(index)
        target = tuple(lax.rem(p + o, n) for p, o, n in zip(place, (ox, oy, oz), counts))
        back = tuple((n - o) % n for o, n in zip((ox, oy, oz), counts))
        row = back[0] * 16
        if not isinstance(row, int):
            row = pl.multiple_of(row, 16)
        return pltpu.make_async_remote_copy(
            src_ref=block,
            dst_ref=all_ref.at[back[1], :, back[2], pl.ds(row, 16), :],
            send_sem=hop_send.at[index],
            recv_sem=hop_recv.at[index],
            device_id=target,
            device_id_type=MESH,
        )

    def hand(index):
        ox, oy, oz = split(index)
        back = tuple((n - o) % n for o, n in zip((ox, oy, oz), counts))
        row = back[0] * 16
        if not isinstance(row, int):
            row = pl.multiple_of(row, 16)
        source = all_ref.at[back[1], :, back[2], pl.ds(row, 16), :]
        if isinstance(index, int) and index == 0:
            source = block
        there = lax.rem(back[2] + nz - 1 + 2 * parity, nz)
        return pltpu.make_async_remote_copy(
            src_ref=source,
            dst_ref=all_ref.at[back[1], :, there, pl.ds(row, 16), :],
            send_sem=pass_send.at[index],
            recv_sem=pass_recv.at[index],
            device_id=partner,
            device_id_type=MESH,
        )

    def each(start, body):
        if chips <= 64:
            for index in range(start, chips):
                body(index)
        else:

            def run(index, carry):
                body(index)
                return carry

            lax.fori_loop(start, chips, run, 0)

    each(1, lambda index: hop(index).start())
    hand(0).start()

    def relay(index):
        hop(index).wait_recv()
        hand(index).start()

    each(1, relay)
    each(1, lambda index: hop(index).wait_send())
    each(0, lambda index: hand(index).wait())


def gather_density(part, counts):
    nx, ny, nz = counts
    chips = nx * ny * nz // 2
    dma = pltpu.SemaphoreType.DMA
    return pl.pallas_call(
        functools.partial(gather_kernel, counts),
        out_shape=jax.ShapeDtypeStruct((ny, 2, nz, 16 * nx, 128), jnp.float32),
        in_specs=[pl.BlockSpec(memory_space=pltpu.VMEM)],
        out_specs=pl.BlockSpec(memory_space=pltpu.VMEM),
        scratch_shapes=[
            pltpu.VMEM((len(OFFSETS), 4, 16, 128), jnp.float32),
            pltpu.VMEM((2, 16, 128), jnp.float32),
            dma((len(OFFSETS),)),
            dma((len(OFFSETS),)),
            dma((chips,)),
            dma((chips,)),
            dma((chips,)),
            dma((chips,)),
        ],
        compiler_params=pltpu.CompilerParams(collective_id=1, has_side_effects=True),
        name="gather",
    )(part)


def basis(extent):
    cells = np.arange(extent)
    columns, waves = [], []
    for wave in range(extent // 2 + 1):
        angle = 2.0 * np.pi * ((cells * wave) % extent) / extent
        single = wave == 0 or 2 * wave == extent
        columns.append(np.cos(angle) * math.sqrt((1.0 if single else 2.0) / extent))
        waves.append(wave)
        if not single:
            columns.append(np.sin(angle) * math.sqrt(2.0 / extent))
            waves.append(wave)
    return np.stack(columns, axis=1), np.array(waves)


def halves_of(table):
    table = jnp.asarray(np.asarray(table, np.float32))
    high = table.astype(jnp.bfloat16)
    low = (table - high.astype(jnp.float32)).astype(jnp.bfloat16)
    return high, low


def numpy_halves(table):
    import ml_dtypes

    table = np.asarray(table, np.float32)
    high = table.astype(ml_dtypes.bfloat16)
    low = (table - high.astype(np.float32)).astype(ml_dtypes.bfloat16)
    return high, low


def tables(counts):
    nx, ny, nz = counts
    qx, wx = basis(16 * nx)
    qy, wy = basis(16 * ny)
    qz, wz = basis(16 * nz)
    mz = np.einsum("icko,gf->igckfo", qz.reshape(nz, 16, nz, 16), np.eye(8))
    y_cells = qy.reshape(ny, 2, 2, 4, 16 * ny).transpose(0, 1, 3, 2, 4)
    my = np.einsum("iplhk,of->iplhokf", y_cells, np.eye(16))
    size_y = 16 * ny * 16
    mz = mz.reshape(nz * 128, nz * 128)
    my = my.reshape(size_y, size_y)

    def wave_term(waves, period):
        return 4.0 / (spacing * spacing) * np.sin(np.pi * waves / period) ** 2

    total = (
        wave_term(wx, 16 * nx)[:, None, None, None]
        + wave_term(wy, 16 * ny)[None, None, :, None]
        + wave_term(wz, 16 * nz).reshape(1, nz, 1, 16)
    )
    return qx, mz, my, total


def split_value(value):
    high = value.astype(jnp.bfloat16)
    low = (value - high.astype(jnp.float32)).astype(jnp.bfloat16)
    return high, low


def product(value, high_ref, low_ref, rows=None):
    high, low = split_value(value)
    if rows is None:
        dims = (((1,), (0,)), ((), ()))
        th, tl = high_ref[...], low_ref[...]
    else:
        dims = (((1,), (1,)), ((), ()))
        th, tl = high_ref[rows, :], low_ref[rows, :]
    dot = functools.partial(
        lax.dot_general, dimension_numbers=dims, preferred_element_type=jnp.float32
    )
    return dot(high, th) + (dot(low, th) + dot(high, tl))


def left_product(high, low, value):
    value_high, value_low = split_value(value)
    dot = functools.partial(jnp.dot, preferred_element_type=jnp.float32)
    return dot(high, value_high) + (dot(high, value_low) + dot(low, value_high))


def exchange_correlation(density):
    positive = density > 0.0
    cube_root = jnp.where(
        positive, jnp.exp(jnp.log(jnp.where(positive, density, 1.0)) * (1.0 / 3.0)), 0.0
    )
    slater = -((3.0 / math.pi) ** (1.0 / 3.0)) * cube_root
    radius = (3.0 / (4.0 * math.pi)) ** (1.0 / 3.0)
    bottom = radius + 7.8 * cube_root
    wigner = -0.44 * cube_root / bottom * (1.0 + radius / (3.0 * bottom))
    return slater + wigner


def window_rows(ref_rows, count):
    return jnp.concatenate([ref_rows(16 * count - 8, 8), ref_rows(0, 24)], axis=0)


def poisson_kernel(counts, all_ref, halo_ref, xh_ref, xl_ref, bh_ref, bl_ref, zh_ref, zl_ref,
                   yh_ref, yl_ref, wave_x, wave_yz, density_ref, potential_ref, modes, back):
    nx, ny, nz = counts
    needed_z = sorted({nz - 1, 0, 1 % nz})
    needed_y = sorted({ny - 1, 0, 1 % ny})

    def run(count, body):
        if count <= 8:
            for index in range(count):
                body(index)
        else:

            def looped(index, carry):
                body(index)
                return carry

            lax.fori_loop(0, count, looped, 0)

    def forward_z(index):
        iy, part = index // 2, index % 2
        value = jnp.concatenate([all_ref[iy, part, iz] for iz in range(nz)], axis=1)
        value = product(value, zh_ref, zl_ref)
        for tile in range(nz):
            modes[tile, index] = value[:, 128 * tile : 128 * tile + 128]

    run(2 * ny, forward_z)

    def middle(tile):
        value = jnp.concatenate([modes[tile, index] for index in range(2 * ny)], axis=1)
        value = product(value, yh_ref, yl_ref)
        value = left_product(xh_ref[...], xl_ref[...], value)
        total = wave_x[...] + wave_yz[tile]
        positive = total > 0.0
        green = jnp.where(positive, 4.0 * math.pi / jnp.where(positive, total, 1.0), 0.0)
        value = left_product(bh_ref[...], bl_ref[...], value * green)
        for iy in needed_y:
            out = product(value, yh_ref, yl_ref, pl.ds(256 * iy, 256))
            for part in range(2):
                back[iy, part, tile] = out[:, 128 * part : 128 * part + 128]

    run(nz, middle)

    cell = lanes((32, 128)) % 32
    for iy in needed_y:
        for part in range(2):
            value = jnp.concatenate([back[iy, part, tile] for tile in range(nz)], axis=1)
            fields = {}
            for iz in needed_z:
                hartree = product(value, zh_ref, zl_ref, pl.ds(128 * iz, 128))
                density = window_rows(
                    lambda start, size: all_ref[iy, part, iz, start : start + size, :], nx
                )
                fields[iz] = hartree + exchange_correlation(density)
            below, own, above = (fields[d % nz] for d in (-1, 0, 1))
            for half in range(2):
                shift = 8 - 16 * half
                value_own = pltpu.roll(own, shift % 128, 1)
                value_below = pltpu.roll(below, (shift - 16) % 128, 1)
                value_above = pltpu.roll(above, (shift + 16) % 128, 1)
                field = jnp.where(
                    cell < 8, value_below, jnp.where(cell < 24, value_own, value_above)
                )
                local = 2 * part + half
                targets = []
                if iy == 0:
                    targets.append(2 + local)
                if iy == (ny - 1) and local >= 2:
                    targets.append(local - 2)
                if iy == 1 % ny and local < 2:
                    targets.append(6 + local)
                for chunk in targets:
                    ion = joined(halo_ref[0, 1, chunk], halo_ref[1, 1, chunk], halo_ref[2, 1, chunk])
                    potential_ref[:, 128 * chunk : 128 * chunk + 128] = ion + field
    for part in range(2):
        merged = all_ref[0, part, 0, 0:16, :]
        for half in range(2):
            for inner in range(4):
                b = 8 * part + 4 * half + inner
                shift = (-(32 * inner + 16 * half)) % 128
                piece = pltpu.roll(merged, shift, 1) if shift else merged
                density_ref[:, b, :] = piece[:, 0:16]


def poisson(everything, windows, counts):
    nx, ny, nz = counts
    qx, mz, my, total = tables(counts)
    window = (np.arange(32) - 8) % (16 * nx)
    wave_x = np.broadcast_to(total[:, 0, 0, 0][:, None], (16 * nx, 128)).astype(np.float32)
    wave_x = np.ascontiguousarray(wave_x[:, :1])
    wave_yz = (total[0] - total[0, 0, 0, 0]).reshape(nz, 1, 16 * ny * 16).astype(np.float32)
    constants = (
        *numpy_halves(qx.T),
        *numpy_halves(qx[window]),
        *numpy_halves(mz),
        *numpy_halves(my),
        wave_x,
        wave_yz,
    )
    vmem = pl.BlockSpec(memory_space=pltpu.VMEM)
    return pl.pallas_call(
        functools.partial(poisson_kernel, counts),
        out_shape=(
            jax.ShapeDtypeStruct((16, 16, 16), jnp.float32),
            jax.ShapeDtypeStruct((32, 1024), jnp.float32),
        ),
        in_specs=[vmem] * (2 + len(constants)),
        out_specs=(vmem, vmem),
        scratch_shapes=[
            pltpu.VMEM((nz, 2 * ny, 16 * nx, 128), jnp.float32),
            pltpu.VMEM((ny, 2, nz, 32, 128), jnp.float32),
        ],
        compiler_params=pltpu.CompilerParams(vmem_limit_bytes=63 * 1024 * 1024),
        name="poisson",
    )(everything, windows, *[jnp.asarray(c) for c in constants])


def on_device(counts, orbitals, potential, ion_potential, occupations):
    fields = jnp.pad(jnp.stack([potential, ion_potential]), ((0, 0), (0, 0), (0, 0), (0, 112)))
    windows = halo(fields, counts)
    new_orbitals, part = filter_orbitals(occupations, orbitals, windows)
    everything = gather_density(part, counts)
    density, new_potential = poisson(everything, windows, counts)
    return (new_orbitals, density, new_potential)


def solution(mesh):
    counts = (mesh.shape["gx"], mesh.shape["gy"], mesh.shape["gz"])
    placed = (P(None, "gx", ("gy", "gz")), P("gx", "gy", "gz"), P("gx", "gy", "gz"), P())
    return jax.shard_map(
        functools.partial(on_device, counts),
        mesh=mesh,
        in_specs=placed,
        out_specs=(P(None, "gx", ("gy", "gz")), P("gx", "gy", "gz"), P("gx", ("gy", "gz"))),
        check_vma=False,
    )
```

```python
import functools
import math

import jax
import jax.numpy as jnp
import numpy as np
from jax import lax
from jax.experimental import pallas as pl
from jax.experimental.pallas import tpu as pltpu
from jax.sharding import PartitionSpec as P

BUF = 8
DEGREE = 10
MESH = pl.DeviceIdType.MESH

spacing = 0.2
kinetic = 0.5 / (spacing * spacing)
filter_low = 6.0
filter_high = 12.0 * kinetic
centre_value = 0.5 * (filter_low + filter_high)
half_width = 0.5 * (filter_high - filter_low)

OFFSETS = [
    (dx, dy, dz)
    for dz in (-1, 0, 1)
    for dx in (-1, 0, 1)
    for dy in (-1, 0, 1)
    if (dx, dy, dz) != (0, 0, 0)
]


def here():
    return lax.axis_index("gx"), lax.axis_index("gy"), lax.axis_index("gz")


def moved(place, offset, counts):
    return tuple(lax.rem(p + (o % n), n) for p, o, n in zip(place, offset, counts))


def distinct(offsets, counts):
    found = []
    for offset in offsets:
        wrapped = tuple(o % n for o, n in zip(offset, counts))
        if any(wrapped) and wrapped not in found:
            found.append(wrapped)
    return found


def greet(offsets, counts):
    barrier = pltpu.get_barrier_semaphore()
    place = here()
    others = distinct(offsets, counts)
    if len(others) <= 64:
        for offset in others:
            pl.semaphore_signal(
                barrier, inc=1, device_id=moved(place, offset, counts), device_id_type=MESH
            )
    else:
        total = counts[0] * counts[1] * counts[2]

        def signal(index, carry):
            offset = (
                index // (counts[1] * counts[2]),
                (index // counts[2]) % counts[1],
                index % counts[2],
            )
            target = tuple(lax.rem(p + o, n) for p, o, n in zip(place, offset, counts))
            pl.semaphore_signal(barrier, inc=1, device_id=target, device_id_type=MESH)
            return carry

        lax.fori_loop(1, total, signal, 0)
    pl.semaphore_wait(barrier, len(others))


def lanes(shape):
    return lax.broadcasted_iota(jnp.int32, shape, len(shape) - 1)


ROWS = {-1: (8, 8, 0), 0: (0, 16, 8), 1: (0, 8, 24)}
PARTS = {-1: (1, 1, 0), 0: (0, 2, 1), 1: (0, 1, 3)}


def halo_kernel(counts, potential_ref, ion_ref, out_ref, wide, block, send_sem, recv_sem):
    place = here()
    wide[0, :, :, 0:16] = potential_ref[...]
    wide[1, :, :, 0:16] = ion_ref[...]
    filled = lanes((16, 128)) < 16
    for field in range(2):
        for part in range(2):
            total = None
            for half in range(2):
                for inner in range(4):
                    piece = wide[field, :, 8 * part + 4 * half + inner, :]
                    piece = jnp.where(filled, piece, 0.0)
                    shift = 32 * inner + 16 * half
                    piece = pltpu.roll(piece, shift, 1) if shift else piece
                    total = piece if total is None else total + piece
            block[field, part] = total
    out_ref[1, :, 1:3, 8:24, :] = block[...]
    greet(OFFSETS, counts)
    copies = []
    for number, (dx, dy, dz) in enumerate(OFFSETS):
        row, rows, to_row = ROWS[dx]
        part, parts, to_part = PARTS[dy]
        copy = pltpu.make_async_remote_copy(
            src_ref=block.at[:, pl.ds(part, parts), pl.ds(row, rows), :],
            dst_ref=out_ref.at[dz + 1, :, pl.ds(to_part, parts), pl.ds(to_row, rows), :],
            send_sem=send_sem.at[number],
            recv_sem=recv_sem.at[number],
            device_id=moved(place, (-dx, -dy, -dz), counts),
            device_id_type=MESH,
        )
        copy.start()
        copies.append(copy)
    for copy in copies:
        copy.wait()


def halo(potential, ion_potential, counts):
    vmem = pl.BlockSpec(memory_space=pltpu.VMEM)
    return pl.pallas_call(
        functools.partial(halo_kernel, counts),
        out_shape=jax.ShapeDtypeStruct((3, 2, 4, 32, 128), jnp.float32),
        in_specs=[vmem, vmem],
        out_specs=vmem,
        scratch_shapes=[
            pltpu.VMEM((2, 16, 16, 128), jnp.float32),
            pltpu.VMEM((2, 2, 16, 128), jnp.float32),
            pltpu.SemaphoreType.DMA((len(OFFSETS),)),
            pltpu.SemaphoreType.DMA((len(OFFSETS),)),
        ],
        compiler_params=pltpu.CompilerParams(collective_id=0, has_side_effects=True),
        name="halo",
    )(potential, ion_potential)


def joined(below, own, above, half):
    cell = lanes(own.shape) % 32
    shift = 8 - 16 * half
    own = pltpu.roll(own, shift % 128, 1)
    below = pltpu.roll(below, (shift - 16) % 128, 1)
    above = pltpu.roll(above, (shift + 16) % 128, 1)
    return jnp.where(cell < 8, below, jnp.where(cell < 24, own, above))


def regrouped(four):
    group = lanes(four[0].shape) // 32
    low, even = group < 2, group % 2 == 0
    turned = [pltpu.roll(v, 64, 1) for v in four]
    four = [
        jnp.where(low, four[0], turned[2]),
        jnp.where(low, four[1], turned[3]),
        jnp.where(low, turned[0], four[2]),
        jnp.where(low, turned[1], four[3]),
    ]
    up = {i: pltpu.roll(four[i], 32, 1) for i in (1, 3)}
    down = {i: pltpu.roll(four[i], 96, 1) for i in (0, 2)}
    return [
        jnp.where(even, four[0], up[1]),
        jnp.where(even, down[0], four[1]),
        jnp.where(even, four[2], up[3]),
        jnp.where(even, down[2], four[3]),
    ]


def ramp(position):
    rising = jnp.clip((position + 0.5 - 0.5 * BUF) / BUF, 0.0, 1.0)
    falling = jnp.clip((32 - 0.5 * BUF - 0.5 - position) / BUF, 0.0, 1.0)
    return rising * falling


def filter_kernel(occ_ref, orbitals_ref, halo_ref, new_ref, part_ref, first, second, diag):
    norb = orbitals_ref.shape[0]
    lane = lanes((32, 128))
    cell = lane % 32
    not_last = cell < 31
    not_first = cell > 0
    inner_up = lane < 96
    inner_down = lane >= 32
    side = kinetic * 2.0 / half_width
    edge = jnp.zeros((8, 128), jnp.float32)

    for odd in range(2):
        fields = [
            joined(halo_ref[0, 0, part], halo_ref[1, 0, part], halo_ref[2, 0, part], odd)
            for part in range(4)
        ]
        for place, field in enumerate(regrouped(fields)):
            diag[4 * odd + place] = (field + (6.0 * kinetic - centre_value)) * (2.0 / half_width)

    def fill(orbital, carry):
        for odd in range(2):
            four = [
                orbitals_ref[orbital, :, 128 * chunk : 128 * chunk + 128].astype(jnp.float32)
                for chunk in range(odd, 8, 2)
            ]
            for place, value in enumerate(regrouped(four)):
                first[orbital, 4 * odd + place, 8:40, :] = value
        for chunk in range(8):
            for ref in (first, second):
                ref[orbital, chunk, 0:8, :] = edge
                ref[orbital, chunk, 40:48, :] = edge
        return carry

    lax.fori_loop(0, norb, fill, 0)

    def step(source, target, start):
        def one(orbital, carry):
            over = jnp.where(inner_up, pltpu.roll(source[orbital, 0, 8:40, :], 96, 1), 0.0)
            under = jnp.where(inner_down, pltpu.roll(source[orbital, 7, 8:40, :], 32, 1), 0.0)
            for chunk in range(8):
                value = source[orbital, chunk, 8:40, :]
                beside = source[orbital, chunk, 7:39, :] + source[orbital, chunk, 9:41, :]
                beside = beside + (source[orbital, chunk + 1, 8:40, :] if chunk < 7 else over)
                beside = beside + (source[orbital, chunk - 1, 8:40, :] if chunk > 0 else under)
                beside = beside + jnp.where(not_last, pltpu.roll(value, 127, 1), 0.0)
                beside = beside + jnp.where(not_first, pltpu.roll(value, 1, 1), 0.0)
                result = diag[chunk] * value - side * beside
                if start:
                    result = 0.5 * result
                else:
                    result = result - target[orbital, chunk, 8:40, :]
                target[orbital, chunk, 8:40, :] = result
            return carry

        lax.fori_loop(0, norb, one, 0)

    step(first, second, True)

    def pair(counter, carry):
        step(second, first, False)
        step(first, second, False)
        return carry

    lax.fori_loop(0, (DEGREE - 1) // 2, pair, 0)
    step(second, first, False)
    filtered = first

    pairs = [(i, j) for i in range(norb) for j in range(i + 1)]

    def gram(index, sums):
        chunk = index // 4
        row = pl.multiple_of(8 + 8 * (index % 4), 8)
        vectors = [filtered[n, chunk, pl.ds(row, 8), :] for n in range(norb)]
        return tuple(s + vectors[i] * vectors[j] for s, (i, j) in zip(sums, pairs))

    zero = jnp.zeros((8, 128), jnp.float32)
    sums = lax.fori_loop(0, 32, gram, (zero,) * len(pairs))
    scale = 1.0 / 32768.0
    matrix = {}
    for key, total in zip(pairs, sums):
        total = jnp.sum(jnp.sum(total, axis=0, keepdims=True), axis=1, keepdims=True)
        matrix[key] = jnp.broadcast_to(total * scale, (8, 128))
    factor = {}
    inverse = {}
    for j in range(norb):
        recip = 1.0 / jnp.sqrt(matrix[(j, j)])
        inverse[(j, j)] = recip
        for i in range(j + 1, norb):
            factor[(i, j)] = matrix[(i, j)] * recip
        for i in range(j + 1, norb):
            for k in range(j + 1, i + 1):
                matrix[(i, k)] = matrix[(i, k)] - factor[(i, j)] * factor[(k, j)]
    for i in range(norb):
        for j in range(i):
            total = None
            for k in range(j, i):
                term = factor[(i, k)] * inverse[(k, j)]
                total = term if total is None else total + term
            inverse[(i, j)] = -total * inverse[(i, i)]
    occ = [jnp.full((8, 128), occ_ref[n], jnp.float32) for n in range(norb)]

    lane8 = lanes((8, 128))
    along_c = ramp((lane8 % 32).astype(jnp.float32))
    row8 = lax.broadcasted_iota(jnp.int32, (8, 128), 0)

    def finish(index, carry):
        chunk, tile = index // 4, index % 4
        row = pl.multiple_of(8 + 8 * tile, 8)
        along_b = ramp((8 * (lane8 // 32) + chunk).astype(jnp.float32))
        along_a = ramp((8 * tile + row8).astype(jnp.float32))
        vectors = [filtered[n, chunk, pl.ds(row, 8), :] for n in range(norb)]
        density = None
        for i in range(norb):
            total = inverse[(i, 0)] * vectors[0]
            for j in range(1, i + 1):
                total = total + inverse[(i, j)] * vectors[j]
            second[i, chunk, pl.ds(row, 8), :] = total
            term = occ[i] * total * total
            density = term if density is None else density + term
        diag[chunk, pl.ds(pl.multiple_of(8 * tile, 8), 8), :] = (
            along_a * (along_b * along_c) * density
        )
        return carry

    lax.fori_loop(0, 32, finish, 0)

    def release(orbital, carry):
        for odd in range(2):
            four = regrouped([second[orbital, 4 * odd + t, 8:40, :] for t in range(4)])
            for place, value in enumerate(four):
                chunk = 2 * place + odd
                new_ref[orbital, :, 128 * chunk : 128 * chunk + 128] = value.astype(jnp.bfloat16)
        return carry

    lax.fori_loop(0, norb, release, 0)
    for odd in range(2):
        four = regrouped([diag[4 * odd + t] for t in range(4)])
        for place, value in enumerate(four):
            part_ref[2 * place + odd] = value


def filter_orbitals(occupations, orbitals, windows):
    norb = orbitals.shape[0]
    return pl.pallas_call(
        filter_kernel,
        out_shape=(
            jax.ShapeDtypeStruct(orbitals.shape, jnp.bfloat16),
            jax.ShapeDtypeStruct((8, 32, 128), jnp.float32),
        ),
        in_specs=[
            pl.BlockSpec(memory_space=pltpu.SMEM),
            pl.BlockSpec(memory_space=pltpu.VMEM),
            pl.BlockSpec(memory_space=pltpu.VMEM),
        ],
        out_specs=(
            pl.BlockSpec(memory_space=pltpu.VMEM),
            pl.BlockSpec(memory_space=pltpu.VMEM),
        ),
        scratch_shapes=[
            pltpu.VMEM((norb, 8, 48, 128), jnp.float32),
            pltpu.VMEM((norb, 8, 48, 128), jnp.float32),
            pltpu.VMEM((8, 32, 128), jnp.float32),
        ],
        name="filter",
    )(occupations, orbitals, windows)


FOLD_ROWS = {-1: (0, 8, 8), 0: (8, 16, 0), 1: (24, 8, 0)}
FOLD_CHUNKS = {-1: (1, 1, 3), 0: (2, 4, 0), 1: (6, 1, 0)}


def gather_kernel(counts, part_ref, all_ref, inbox, block, send_sem, recv_sem, hop_send, hop_recv,
                  pass_send, pass_recv):
    nx, ny, nz = counts
    place = here()
    everyone = [(x, y, z) for x in range(nx) for y in range(ny) for z in range(nz)]
    greet(everyone, counts)
    copies = []
    for number, (dx, dy, dz) in enumerate(OFFSETS):
        row, rows, _ = FOLD_ROWS[dx]
        chunk, chunks, _ = FOLD_CHUNKS[dy]
        copy = pltpu.make_async_remote_copy(
            src_ref=part_ref.at[pl.ds(chunk, chunks), pl.ds(row, rows), :],
            dst_ref=inbox.at[number, pl.ds(0, chunks), pl.ds(0, rows), :],
            send_sem=send_sem.at[number],
            recv_sem=recv_sem.at[number],
            device_id=moved(place, (dx, dy, dz), counts),
            device_id_type=MESH,
        )
        copy.start()
        copies.append(copy)
    for copy in copies:
        copy.wait()
    cell = lanes((16, 128)) % 32
    sums = {}
    for chunk in range(4):
        for dz in (-1, 0, 1):
            low = part_ref[2 + chunk, 8:16, :] if dz == 0 else jnp.zeros((8, 128), jnp.float32)
            high = part_ref[2 + chunk, 16:24, :] if dz == 0 else jnp.zeros((8, 128), jnp.float32)
            for number, (dx, dy, other) in enumerate(OFFSETS):
                if other != dz:
                    continue
                _, chunks, to_chunk = FOLD_CHUNKS[dy]
                if not to_chunk <= chunk < to_chunk + chunks:
                    continue
                at = chunk - to_chunk
                if dx == 0:
                    low = low + inbox[number, at, 0:8, :]
                    high = high + inbox[number, at, 8:16, :]
                elif dx == 1:
                    low = low + inbox[number, at, 0:8, :]
                else:
                    high = high + inbox[number, at, 0:8, :]
            total = jnp.concatenate([low, high], axis=0)
            if dz == 1:
                total = jnp.where((cell >= 8) & (cell < 12), pltpu.roll(total, 112, 1), 0.0)
            elif dz == -1:
                total = jnp.where((cell >= 20) & (cell < 24), pltpu.roll(total, 16, 1), 0.0)
            sums[chunk] = total if dz == -1 else sums[chunk] + total
    for part in range(2):
        merged = jnp.where(
            cell < 16, pltpu.roll(sums[2 * part], 120, 1), pltpu.roll(sums[2 * part + 1], 8, 1)
        )
        block[part] = merged
        all_ref[0, part, 0, 0:16, :] = merged

    parity = lax.rem(place[2], 2)
    partner = (place[0], place[1], place[2] + 1 - 2 * parity)
    pairs = nz // 2
    chips = nx * ny * pairs

    def split(index):
        return index // (ny * pairs), (index // pairs) % ny, 2 * (index % pairs)

    def hop(index):
        ox, oy, oz = split(index)
        target = tuple(lax.rem(p + o, n) for p, o, n in zip(place, (ox, oy, oz), counts))
        back = tuple((n - o) % n for o, n in zip((ox, oy, oz), counts))
        row = back[0] * 16
        if not isinstance(row, int):
            row = pl.multiple_of(row, 16)
        return pltpu.make_async_remote_copy(
            src_ref=block,
            dst_ref=all_ref.at[back[1], :, back[2], pl.ds(row, 16), :],
            send_sem=hop_send.at[index],
            recv_sem=hop_recv.at[index],
            device_id=target,
            device_id_type=MESH,
        )

    def hand(index):
        ox, oy, oz = split(index)
        back = tuple((n - o) % n for o, n in zip((ox, oy, oz), counts))
        row = back[0] * 16
        if not isinstance(row, int):
            row = pl.multiple_of(row, 16)
        source = all_ref.at[back[1], :, back[2], pl.ds(row, 16), :]
        if isinstance(index, int) and index == 0:
            source = block
        there = lax.rem(back[2] + nz - 1 + 2 * parity, nz)
        return pltpu.make_async_remote_copy(
            src_ref=source,
            dst_ref=all_ref.at[back[1], :, there, pl.ds(row, 16), :],
            send_sem=pass_send.at[index],
            recv_sem=pass_recv.at[index],
            device_id=partner,
            device_id_type=MESH,
        )

    def each(start, body):
        if chips <= 64:
            for index in range(start, chips):
                body(index)
        else:

            def run(index, carry):
                body(index)
                return carry

            lax.fori_loop(start, chips, run, 0)

    each(1, lambda index: hop(index).start())
    hand(0).start()

    def relay(index):
        hop(index).wait_recv()
        hand(index).start()

    each(1, relay)
    each(1, lambda index: hop(index).wait_send())
    each(0, lambda index: hand(index).wait())


def gather_density(part, counts):
    nx, ny, nz = counts
    chips = nx * ny * nz // 2
    dma = pltpu.SemaphoreType.DMA
    return pl.pallas_call(
        functools.partial(gather_kernel, counts),
        out_shape=jax.ShapeDtypeStruct((ny, 2, nz, 16 * nx, 128), jnp.float32),
        in_specs=[pl.BlockSpec(memory_space=pltpu.VMEM)],
        out_specs=pl.BlockSpec(memory_space=pltpu.VMEM),
        scratch_shapes=[
            pltpu.VMEM((len(OFFSETS), 4, 16, 128), jnp.float32),
            pltpu.VMEM((2, 16, 128), jnp.float32),
            dma((len(OFFSETS),)),
            dma((len(OFFSETS),)),
            dma((chips,)),
            dma((chips,)),
            dma((chips,)),
            dma((chips,)),
        ],
        compiler_params=pltpu.CompilerParams(collective_id=1, has_side_effects=True),
        name="gather",
    )(part)


def basis(extent):
    cells = np.arange(extent)
    columns, waves = [], []
    for wave in range(extent // 2 + 1):
        angle = 2.0 * np.pi * ((cells * wave) % extent) / extent
        single = wave == 0 or 2 * wave == extent
        columns.append(np.cos(angle) * math.sqrt((1.0 if single else 2.0) / extent))
        waves.append(wave)
        if not single:
            columns.append(np.sin(angle) * math.sqrt(2.0 / extent))
            waves.append(wave)
    return np.stack(columns, axis=1), np.array(waves)


def halves_of(table):
    table = jnp.asarray(np.asarray(table, np.float32))
    high = table.astype(jnp.bfloat16)
    low = (table - high.astype(jnp.float32)).astype(jnp.bfloat16)
    return high, low


def numpy_halves(table):
    import ml_dtypes

    table = np.asarray(table, np.float32)
    high = table.astype(ml_dtypes.bfloat16)
    low = (table - high.astype(np.float32)).astype(ml_dtypes.bfloat16)
    return high, low


def tables(counts):
    nx, ny, nz = counts
    qx, wx = basis(16 * nx)
    qy, wy = basis(16 * ny)
    qz, wz = basis(16 * nz)
    mz = np.einsum("icko,gf->igckfo", qz.reshape(nz, 16, nz, 16), np.eye(8))
    y_cells = qy.reshape(ny, 2, 2, 4, 16 * ny).transpose(0, 1, 3, 2, 4)
    my = np.einsum("iplhk,of->iplhokf", y_cells, np.eye(16))
    size_y = 16 * ny * 16
    mz = mz.reshape(nz * 128, nz * 128)
    my = my.reshape(size_y, size_y)

    def wave_term(waves, period):
        return 4.0 / (spacing * spacing) * np.sin(np.pi * waves / period) ** 2

    total = (
        wave_term(wx, 16 * nx)[:, None, None, None]
        + wave_term(wy, 16 * ny)[None, None, :, None]
        + wave_term(wz, 16 * nz).reshape(1, nz, 1, 16)
    )
    return qx, mz, my, total


def split_value(value):
    high = value.astype(jnp.bfloat16)
    low = (value - high.astype(jnp.float32)).astype(jnp.bfloat16)
    return high, low


def product(value, high_ref, low_ref, rows=None):
    high, low = split_value(value)
    if rows is None:
        dims = (((1,), (0,)), ((), ()))
        th, tl = high_ref[...], low_ref[...]
    else:
        dims = (((1,), (1,)), ((), ()))
        th, tl = high_ref[rows, :], low_ref[rows, :]
    dot = functools.partial(
        lax.dot_general, dimension_numbers=dims, preferred_element_type=jnp.float32
    )
    return dot(high, th) + (dot(low, th) + dot(high, tl))


def left_product(high, low, value):
    value_high, value_low = split_value(value)
    dot = functools.partial(jnp.dot, preferred_element_type=jnp.float32)
    return dot(high, value_high) + (dot(high, value_low) + dot(low, value_high))


def exchange_correlation(density):
    positive = density > 0.0
    cube_root = jnp.where(
        positive, jnp.exp(jnp.log(jnp.where(positive, density, 1.0)) * (1.0 / 3.0)), 0.0
    )
    slater = -((3.0 / math.pi) ** (1.0 / 3.0)) * cube_root
    radius = (3.0 / (4.0 * math.pi)) ** (1.0 / 3.0)
    bottom = radius + 7.8 * cube_root
    wigner = -0.44 * cube_root / bottom * (1.0 + radius / (3.0 * bottom))
    return slater + wigner


def window_rows(ref_rows, count):
    return jnp.concatenate([ref_rows(16 * count - 8, 8), ref_rows(0, 24)], axis=0)


def poisson_kernel(counts, all_ref, halo_ref, xh_ref, xl_ref, bh_ref, bl_ref, zh_ref, zl_ref,
                   yh_ref, yl_ref, wave_x, wave_yz, density_ref, potential_ref, modes, back):
    nx, ny, nz = counts
    needed_z = sorted({nz - 1, 0, 1 % nz})
    needed_y = sorted({ny - 1, 0, 1 % ny})

    def run(count, body):
        if count <= 8:
            for index in range(count):
                body(index)
        else:

            def looped(index, carry):
                body(index)
                return carry

            lax.fori_loop(0, count, looped, 0)

    def forward_z(index):
        iy, part = index // 2, index % 2
        value = jnp.concatenate([all_ref[iy, part, iz] for iz in range(nz)], axis=1)
        value = product(value, zh_ref, zl_ref)
        for tile in range(nz):
            modes[tile, index] = value[:, 128 * tile : 128 * tile + 128]

    run(2 * ny, forward_z)

    def middle(tile):
        value = jnp.concatenate([modes[tile, index] for index in range(2 * ny)], axis=1)
        value = product(value, yh_ref, yl_ref)
        value = left_product(xh_ref[...], xl_ref[...], value)
        total = wave_x[...] + wave_yz[tile]
        positive = total > 0.0
        green = jnp.where(positive, 4.0 * math.pi / jnp.where(positive, total, 1.0), 0.0)
        value = left_product(bh_ref[...], bl_ref[...], value * green)
        for iy in needed_y:
            out = product(value, yh_ref, yl_ref, pl.ds(256 * iy, 256))
            for part in range(2):
                back[iy, part, tile] = out[:, 128 * part : 128 * part + 128]

    run(nz, middle)

    for iy in needed_y:
        for part in range(2):
            value = jnp.concatenate([back[iy, part, tile] for tile in range(nz)], axis=1)
            fields = {}
            for iz in needed_z:
                hartree = product(value, zh_ref, zl_ref, pl.ds(128 * iz, 128))
                density = window_rows(
                    lambda start, size: all_ref[iy, part, iz, start : start + size, :], nx
                )
                fields[iz] = hartree + exchange_correlation(density)
            below, own, above = (fields[d % nz] for d in (-1, 0, 1))
            for half in range(2):
                field = joined(below, own, above, half)
                local = 2 * part + half
                targets = []
                if iy == 0:
                    targets.append(2 + local)
                if iy == (ny - 1) and local >= 2:
                    targets.append(local - 2)
                if iy == 1 % ny and local < 2:
                    targets.append(6 + local)
                for chunk in targets:
                    ion = joined(*[halo_ref[d, 1, chunk // 2] for d in range(3)], half)
                    potential_ref[:, 128 * chunk : 128 * chunk + 128] = ion + field
    for part in range(2):
        merged = all_ref[0, part, 0, 0:16, :]
        for half in range(2):
            for inner in range(4):
                b = 8 * part + 4 * half + inner
                shift = (-(32 * inner + 16 * half)) % 128
                piece = pltpu.roll(merged, shift, 1) if shift else merged
                density_ref[:, b, :] = piece[:, 0:16]


def poisson(everything, windows, counts):
    nx, ny, nz = counts
    qx, mz, my, total = tables(counts)
    window = (np.arange(32) - 8) % (16 * nx)
    wave_x = np.broadcast_to(total[:, 0, 0, 0][:, None], (16 * nx, 128)).astype(np.float32)
    wave_x = np.ascontiguousarray(wave_x[:, :1])
    wave_yz = (total[0] - total[0, 0, 0, 0]).reshape(nz, 1, 16 * ny * 16).astype(np.float32)
    constants = (
        *numpy_halves(qx.T),
        *numpy_halves(qx[window]),
        *numpy_halves(mz),
        *numpy_halves(my),
        wave_x,
        wave_yz,
    )
    vmem = pl.BlockSpec(memory_space=pltpu.VMEM)
    return pl.pallas_call(
        functools.partial(poisson_kernel, counts),
        out_shape=(
            jax.ShapeDtypeStruct((16, 16, 16), jnp.float32),
            jax.ShapeDtypeStruct((32, 1024), jnp.float32),
        ),
        in_specs=[vmem] * (2 + len(constants)),
        out_specs=(vmem, vmem),
        scratch_shapes=[
            pltpu.VMEM((nz, 2 * ny, 16 * nx, 128), jnp.float32),
            pltpu.VMEM((ny, 2, nz, 32, 128), jnp.float32),
        ],
        compiler_params=pltpu.CompilerParams(vmem_limit_bytes=63 * 1024 * 1024),
        name="poisson",
    )(everything, windows, *[jnp.asarray(c) for c in constants])


def on_device(counts, orbitals, potential, ion_potential, occupations):
    windows = halo(potential, ion_potential, counts)
    new_orbitals, part = filter_orbitals(occupations, orbitals, windows)
    everything = gather_density(part, counts)
    density, new_potential = poisson(everything, windows, counts)
    return (new_orbitals, density, new_potential)


def solution(mesh):
    counts = (mesh.shape["gx"], mesh.shape["gy"], mesh.shape["gz"])
    placed = (P(None, "gx", ("gy", "gz")), P("gx", "gy", "gz"), P("gx", "gy", "gz"), P())
    return jax.shard_map(
        functools.partial(on_device, counts),
        mesh=mesh,
        in_specs=placed,
        out_specs=(P(None, "gx", ("gy", "gz")), P("gx", "gy", "gz"), P("gx", ("gy", "gz"))),
        check_vma=False,
    )
```

```python
import functools
import math

import jax
import jax.numpy as jnp
import numpy as np
from jax import lax
from jax.experimental import pallas as pl
from jax.experimental.pallas import tpu as pltpu
from jax.sharding import PartitionSpec as P

BUF = 8
DEGREE = 10
MESH = pl.DeviceIdType.MESH

spacing = 0.2
kinetic = 0.5 / (spacing * spacing)
filter_low = 6.0
filter_high = 12.0 * kinetic
centre_value = 0.5 * (filter_low + filter_high)
half_width = 0.5 * (filter_high - filter_low)

OFFSETS = [
    (dx, dy, dz)
    for dz in (-1, 0, 1)
    for dx in (-1, 0, 1)
    for dy in (-1, 0, 1)
    if (dx, dy, dz) != (0, 0, 0)
]


def here():
    return lax.axis_index("gx"), lax.axis_index("gy"), lax.axis_index("gz")


def moved(place, offset, counts):
    return tuple(lax.rem(p + (o % n), n) for p, o, n in zip(place, offset, counts))


def distinct(offsets, counts):
    found = []
    for offset in offsets:
        wrapped = tuple(o % n for o, n in zip(offset, counts))
        if any(wrapped) and wrapped not in found:
            found.append(wrapped)
    return found


def greet(offsets, counts):
    barrier = pltpu.get_barrier_semaphore()
    place = here()
    others = distinct(offsets, counts)
    if len(others) <= 64:
        for offset in others:
            pl.semaphore_signal(
                barrier, inc=1, device_id=moved(place, offset, counts), device_id_type=MESH
            )
    else:
        total = counts[0] * counts[1] * counts[2]

        def signal(index, carry):
            offset = (
                index // (counts[1] * counts[2]),
                (index // counts[2]) % counts[1],
                index % counts[2],
            )
            target = tuple(lax.rem(p + o, n) for p, o, n in zip(place, offset, counts))
            pl.semaphore_signal(barrier, inc=1, device_id=target, device_id_type=MESH)
            return carry

        lax.fori_loop(1, total, signal, 0)
    pl.semaphore_wait(barrier, len(others))


def lanes(shape):
    return lax.broadcasted_iota(jnp.int32, shape, len(shape) - 1)


ROWS = {-1: (8, 8, 0), 0: (0, 16, 8), 1: (0, 8, 24)}
PARTS = {-1: (1, 1, 0), 0: (0, 2, 1), 1: (0, 1, 3)}


def halo_kernel(counts, potential_ref, ion_ref, out_ref, wide, block, send_sem, recv_sem):
    place = here()
    wide[0, :, :, 0:16] = potential_ref[...]
    wide[1, :, :, 0:16] = ion_ref[...]
    filled = lanes((16, 128)) < 16
    for field in range(2):
        for part in range(2):
            total = None
            for half in range(2):
                for inner in range(4):
                    piece = wide[field, :, 8 * part + 4 * half + inner, :]
                    piece = jnp.where(filled, piece, 0.0)
                    shift = 32 * inner + 16 * half
                    piece = pltpu.roll(piece, shift, 1) if shift else piece
                    total = piece if total is None else total + piece
            block[field, part] = total
    out_ref[1, :, 1:3, 8:24, :] = block[...]
    greet(OFFSETS, counts)
    copies = []
    for number, (dx, dy, dz) in enumerate(OFFSETS):
        row, rows, to_row = ROWS[dx]
        part, parts, to_part = PARTS[dy]
        copy = pltpu.make_async_remote_copy(
            src_ref=block.at[:, pl.ds(part, parts), pl.ds(row, rows), :],
            dst_ref=out_ref.at[dz + 1, :, pl.ds(to_part, parts), pl.ds(to_row, rows), :],
            send_sem=send_sem.at[number],
            recv_sem=recv_sem.at[number],
            device_id=moved(place, (-dx, -dy, -dz), counts),
            device_id_type=MESH,
        )
        copy.start()
        copies.append(copy)
    for copy in copies:
        copy.wait()


def halo(potential, ion_potential, counts):
    vmem = pl.BlockSpec(memory_space=pltpu.VMEM)
    return pl.pallas_call(
        functools.partial(halo_kernel, counts),
        out_shape=jax.ShapeDtypeStruct((3, 2, 4, 32, 128), jnp.float32),
        in_specs=[vmem, vmem],
        out_specs=vmem,
        scratch_shapes=[
            pltpu.VMEM((2, 16, 16, 128), jnp.float32),
            pltpu.VMEM((2, 2, 16, 128), jnp.float32),
            pltpu.SemaphoreType.DMA((len(OFFSETS),)),
            pltpu.SemaphoreType.DMA((len(OFFSETS),)),
        ],
        compiler_params=pltpu.CompilerParams(collective_id=0, has_side_effects=True),
        name="halo",
    )(potential, ion_potential)


def joined(below, own, above, half):
    cell = lanes(own.shape) % 32
    shift = 8 - 16 * half
    own = pltpu.roll(own, shift % 128, 1)
    below = pltpu.roll(below, (shift - 16) % 128, 1)
    above = pltpu.roll(above, (shift + 16) % 128, 1)
    return jnp.where(cell < 8, below, jnp.where(cell < 24, own, above))


def regrouped(four):
    group = lanes(four[0].shape) // 32
    low, even = group < 2, group % 2 == 0
    turned = [pltpu.roll(v, 64, 1) for v in four]
    four = [
        jnp.where(low, four[0], turned[2]),
        jnp.where(low, four[1], turned[3]),
        jnp.where(low, turned[0], four[2]),
        jnp.where(low, turned[1], four[3]),
    ]
    up = {i: pltpu.roll(four[i], 32, 1) for i in (1, 3)}
    down = {i: pltpu.roll(four[i], 96, 1) for i in (0, 2)}
    return [
        jnp.where(even, four[0], up[1]),
        jnp.where(even, down[0], four[1]),
        jnp.where(even, four[2], up[3]),
        jnp.where(even, down[2], four[3]),
    ]


def ramp(position):
    rising = jnp.clip((position + 0.5 - 0.5 * BUF) / BUF, 0.0, 1.0)
    falling = jnp.clip((32 - 0.5 * BUF - 0.5 - position) / BUF, 0.0, 1.0)
    return rising * falling


def filter_kernel(occ_ref, orbitals_ref, halo_ref, new_ref, part_ref, first, second, diag):
    norb = orbitals_ref.shape[0]
    lane = lanes((32, 128))
    cell = lane % 32
    not_last = cell < 31
    not_first = cell > 0
    inner_up = lane < 96
    inner_down = lane >= 32
    side = kinetic * 2.0 / half_width
    edge = jnp.zeros((8, 128), jnp.float32)

    for odd in range(2):
        fields = [
            joined(halo_ref[0, 0, part], halo_ref[1, 0, part], halo_ref[2, 0, part], odd)
            for part in range(4)
        ]
        for place, field in enumerate(regrouped(fields)):
            diag[4 * odd + place] = (field + (6.0 * kinetic - centre_value)) * (2.0 / half_width)

    def fill(orbital, carry):
        for odd in range(2):
            four = [
                orbitals_ref[orbital, :, 128 * chunk : 128 * chunk + 128].astype(jnp.float32)
                for chunk in range(odd, 8, 2)
            ]
            for place, value in enumerate(regrouped(four)):
                first[orbital, 4 * odd + place, 8:40, :] = value
        for chunk in range(8):
            for ref in (first, second):
                ref[orbital, chunk, 0:8, :] = edge
                ref[orbital, chunk, 40:48, :] = edge
        return carry

    lax.fori_loop(0, norb, fill, 0)

    def step(source, target, start):
        size = 4 if norb % 4 == 0 else 1

        def one(group, carry):
            members = [size * group + m for m in range(size)]
            overs, unders = {}, {}
            for m, orbital in enumerate(members):
                over = pltpu.roll(source[orbital, 0, 8:40, :], 96, 1)
                under = pltpu.roll(source[orbital, 7, 8:40, :], 32, 1)
                overs[m] = jnp.where(inner_up, over, 0.0)
                unders[m] = jnp.where(inner_down, under, 0.0)
            for chunk, m in [(c, m) for m in range(len(members)) for c in range(8)]:
                orbital, over, under = members[m], overs[m], unders[m]
                value = source[orbital, chunk, 8:40, :]
                beside = source[orbital, chunk, 7:39, :] + source[orbital, chunk, 9:41, :]
                beside = beside + (source[orbital, chunk + 1, 8:40, :] if chunk < 7 else over)
                beside = beside + (source[orbital, chunk - 1, 8:40, :] if chunk > 0 else under)
                beside = beside + jnp.where(not_last, pltpu.roll(value, 127, 1), 0.0)
                beside = beside + jnp.where(not_first, pltpu.roll(value, 1, 1), 0.0)
                result = diag[chunk] * value - side * beside
                if start:
                    result = 0.5 * result
                else:
                    result = result - target[orbital, chunk, 8:40, :]
                target[orbital, chunk, 8:40, :] = result
            return carry

        lax.fori_loop(0, norb // size, one, 0)

    step(first, second, True)

    def pair(counter, carry):
        step(second, first, False)
        step(first, second, False)
        return carry

    lax.fori_loop(0, (DEGREE - 1) // 2, pair, 0)
    step(second, first, False)
    filtered = first

    pairs = [(i, j) for i in range(norb) for j in range(i + 1)]

    def gram(index, sums):
        chunk = index // 4
        row = pl.multiple_of(8 + 8 * (index % 4), 8)
        vectors = [filtered[n, chunk, pl.ds(row, 8), :] for n in range(norb)]
        return tuple(s + vectors[i] * vectors[j] for s, (i, j) in zip(sums, pairs))

    zero = jnp.zeros((8, 128), jnp.float32)
    sums = lax.fori_loop(0, 32, gram, (zero,) * len(pairs))
    scale = 1.0 / 32768.0
    matrix = {}
    for key, total in zip(pairs, sums):
        total = jnp.sum(jnp.sum(total, axis=0, keepdims=True), axis=1, keepdims=True)
        matrix[key] = jnp.broadcast_to(total * scale, (8, 128))
    factor = {}
    inverse = {}
    for j in range(norb):
        recip = 1.0 / jnp.sqrt(matrix[(j, j)])
        inverse[(j, j)] = recip
        for i in range(j + 1, norb):
            factor[(i, j)] = matrix[(i, j)] * recip
        for i in range(j + 1, norb):
            for k in range(j + 1, i + 1):
                matrix[(i, k)] = matrix[(i, k)] - factor[(i, j)] * factor[(k, j)]
    for i in range(norb):
        for j in range(i):
            total = None
            for k in range(j, i):
                term = factor[(i, k)] * inverse[(k, j)]
                total = term if total is None else total + term
            inverse[(i, j)] = -total * inverse[(i, i)]
    occ = [jnp.full((8, 128), occ_ref[n], jnp.float32) for n in range(norb)]

    lane8 = lanes((8, 128))
    along_c = ramp((lane8 % 32).astype(jnp.float32))
    row8 = lax.broadcasted_iota(jnp.int32, (8, 128), 0)

    def finish(index, carry):
        chunk, tile = index // 4, index % 4
        row = pl.multiple_of(8 + 8 * tile, 8)
        along_b = ramp((8 * (lane8 // 32) + chunk).astype(jnp.float32))
        along_a = ramp((8 * tile + row8).astype(jnp.float32))
        vectors = [filtered[n, chunk, pl.ds(row, 8), :] for n in range(norb)]
        density = None
        for i in range(norb):
            total = inverse[(i, 0)] * vectors[0]
            for j in range(1, i + 1):
                total = total + inverse[(i, j)] * vectors[j]
            second[i, chunk, pl.ds(row, 8), :] = total
            term = occ[i] * total * total
            density = term if density is None else density + term
        diag[chunk, pl.ds(pl.multiple_of(8 * tile, 8), 8), :] = (
            along_a * (along_b * along_c) * density
        )
        return carry

    lax.fori_loop(0, 32, finish, 0)

    def release(orbital, carry):
        for odd in range(2):
            four = regrouped([second[orbital, 4 * odd + t, 8:40, :] for t in range(4)])
            for place, value in enumerate(four):
                chunk = 2 * place + odd
                new_ref[orbital, :, 128 * chunk : 128 * chunk + 128] = value.astype(jnp.bfloat16)
        return carry

    lax.fori_loop(0, norb, release, 0)
    for odd in range(2):
        four = regrouped([diag[4 * odd + t] for t in range(4)])
        for place, value in enumerate(four):
            part_ref[2 * place + odd] = value


def filter_orbitals(occupations, orbitals, windows):
    norb = orbitals.shape[0]
    return pl.pallas_call(
        filter_kernel,
        out_shape=(
            jax.ShapeDtypeStruct(orbitals.shape, jnp.bfloat16),
            jax.ShapeDtypeStruct((8, 32, 128), jnp.float32),
        ),
        in_specs=[
            pl.BlockSpec(memory_space=pltpu.SMEM),
            pl.BlockSpec(memory_space=pltpu.VMEM),
            pl.BlockSpec(memory_space=pltpu.VMEM),
        ],
        out_specs=(
            pl.BlockSpec(memory_space=pltpu.VMEM),
            pl.BlockSpec(memory_space=pltpu.VMEM),
        ),
        scratch_shapes=[
            pltpu.VMEM((norb, 8, 48, 128), jnp.float32),
            pltpu.VMEM((norb, 8, 48, 128), jnp.float32),
            pltpu.VMEM((8, 32, 128), jnp.float32),
        ],
        name="filter",
    )(occupations, orbitals, windows)


FOLD_ROWS = {-1: (0, 8, 8), 0: (8, 16, 0), 1: (24, 8, 0)}
FOLD_CHUNKS = {-1: (1, 1, 3), 0: (2, 4, 0), 1: (6, 1, 0)}


def gather_kernel(counts, part_ref, all_ref, inbox, block, send_sem, recv_sem, hop_send, hop_recv,
                  pass_send, pass_recv):
    nx, ny, nz = counts
    place = here()
    everyone = [(x, y, z) for x in range(nx) for y in range(ny) for z in range(nz)]
    greet(everyone, counts)
    copies = []
    for number, (dx, dy, dz) in enumerate(OFFSETS):
        row, rows, _ = FOLD_ROWS[dx]
        chunk, chunks, _ = FOLD_CHUNKS[dy]
        copy = pltpu.make_async_remote_copy(
            src_ref=part_ref.at[pl.ds(chunk, chunks), pl.ds(row, rows), :],
            dst_ref=inbox.at[number, pl.ds(0, chunks), pl.ds(0, rows), :],
            send_sem=send_sem.at[number],
            recv_sem=recv_sem.at[number],
            device_id=moved(place, (dx, dy, dz), counts),
            device_id_type=MESH,
        )
        copy.start()
        copies.append(copy)
    for copy in copies:
        copy.wait()
    cell = lanes((16, 128)) % 32
    sums = {}
    for chunk in range(4):
        for dz in (-1, 0, 1):
            low = part_ref[2 + chunk, 8:16, :] if dz == 0 else jnp.zeros((8, 128), jnp.float32)
            high = part_ref[2 + chunk, 16:24, :] if dz == 0 else jnp.zeros((8, 128), jnp.float32)
            for number, (dx, dy, other) in enumerate(OFFSETS):
                if other != dz:
                    continue
                _, chunks, to_chunk = FOLD_CHUNKS[dy]
                if not to_chunk <= chunk < to_chunk + chunks:
                    continue
                at = chunk - to_chunk
                if dx == 0:
                    low = low + inbox[number, at, 0:8, :]
                    high = high + inbox[number, at, 8:16, :]
                elif dx == 1:
                    low = low + inbox[number, at, 0:8, :]
                else:
                    high = high + inbox[number, at, 0:8, :]
            total = jnp.concatenate([low, high], axis=0)
            if dz == 1:
                total = jnp.where((cell >= 8) & (cell < 12), pltpu.roll(total, 112, 1), 0.0)
            elif dz == -1:
                total = jnp.where((cell >= 20) & (cell < 24), pltpu.roll(total, 16, 1), 0.0)
            sums[chunk] = total if dz == -1 else sums[chunk] + total
    for part in range(2):
        merged = jnp.where(
            cell < 16, pltpu.roll(sums[2 * part], 120, 1), pltpu.roll(sums[2 * part + 1], 8, 1)
        )
        block[part] = merged
        all_ref[0, part, 0, 0:16, :] = merged

    parity = lax.rem(place[2], 2)
    partner = (place[0], place[1], place[2] + 1 - 2 * parity)
    pairs = nz // 2
    chips = nx * ny * pairs

    def split(index):
        return index // (ny * pairs), (index // pairs) % ny, 2 * (index % pairs)

    def hop(index):
        ox, oy, oz = split(index)
        target = tuple(lax.rem(p + o, n) for p, o, n in zip(place, (ox, oy, oz), counts))
        back = tuple((n - o) % n for o, n in zip((ox, oy, oz), counts))
        row = back[0] * 16
        if not isinstance(row, int):
            row = pl.multiple_of(row, 16)
        return pltpu.make_async_remote_copy(
            src_ref=block,
            dst_ref=all_ref.at[back[1], :, back[2], pl.ds(row, 16), :],
            send_sem=hop_send.at[index],
            recv_sem=hop_recv.at[index],
            device_id=target,
            device_id_type=MESH,
        )

    def hand(index):
        ox, oy, oz = split(index)
        back = tuple((n - o) % n for o, n in zip((ox, oy, oz), counts))
        row = back[0] * 16
        if not isinstance(row, int):
            row = pl.multiple_of(row, 16)
        source = all_ref.at[back[1], :, back[2], pl.ds(row, 16), :]
        if isinstance(index, int) and index == 0:
            source = block
        there = lax.rem(back[2] + nz - 1 + 2 * parity, nz)
        return pltpu.make_async_remote_copy(
            src_ref=source,
            dst_ref=all_ref.at[back[1], :, there, pl.ds(row, 16), :],
            send_sem=pass_send.at[index],
            recv_sem=pass_recv.at[index],
            device_id=partner,
            device_id_type=MESH,
        )

    def each(start, body):
        if chips <= 64:
            for index in range(start, chips):
                body(index)
        else:

            def run(index, carry):
                body(index)
                return carry

            lax.fori_loop(start, chips, run, 0)

    each(1, lambda index: hop(index).start())
    hand(0).start()

    def relay(index):
        hop(index).wait_recv()
        hand(index).start()

    each(1, relay)
    each(1, lambda index: hop(index).wait_send())
    each(0, lambda index: hand(index).wait())


def gather_density(part, counts):
    nx, ny, nz = counts
    chips = nx * ny * nz // 2
    dma = pltpu.SemaphoreType.DMA
    return pl.pallas_call(
        functools.partial(gather_kernel, counts),
        out_shape=jax.ShapeDtypeStruct((ny, 2, nz, 16 * nx, 128), jnp.float32),
        in_specs=[pl.BlockSpec(memory_space=pltpu.VMEM)],
        out_specs=pl.BlockSpec(memory_space=pltpu.VMEM),
        scratch_shapes=[
            pltpu.VMEM((len(OFFSETS), 4, 16, 128), jnp.float32),
            pltpu.VMEM((2, 16, 128), jnp.float32),
            dma((len(OFFSETS),)),
            dma((len(OFFSETS),)),
            dma((chips,)),
            dma((chips,)),
            dma((chips,)),
            dma((chips,)),
        ],
        compiler_params=pltpu.CompilerParams(collective_id=1, has_side_effects=True),
        name="gather",
    )(part)


def basis(extent):
    cells = np.arange(extent)
    columns, waves = [], []
    for wave in range(extent // 2 + 1):
        angle = 2.0 * np.pi * ((cells * wave) % extent) / extent
        single = wave == 0 or 2 * wave == extent
        columns.append(np.cos(angle) * math.sqrt((1.0 if single else 2.0) / extent))
        waves.append(wave)
        if not single:
            columns.append(np.sin(angle) * math.sqrt(2.0 / extent))
            waves.append(wave)
    return np.stack(columns, axis=1), np.array(waves)


def halves_of(table):
    table = jnp.asarray(np.asarray(table, np.float32))
    high = table.astype(jnp.bfloat16)
    low = (table - high.astype(jnp.float32)).astype(jnp.bfloat16)
    return high, low


def numpy_halves(table):
    import ml_dtypes

    table = np.asarray(table, np.float32)
    high = table.astype(ml_dtypes.bfloat16)
    low = (table - high.astype(np.float32)).astype(ml_dtypes.bfloat16)
    return high, low


def tables(counts):
    nx, ny, nz = counts
    qx, wx = basis(16 * nx)
    qy, wy = basis(16 * ny)
    qz, wz = basis(16 * nz)
    mz = np.einsum("icko,gf->igckfo", qz.reshape(nz, 16, nz, 16), np.eye(8))
    y_cells = qy.reshape(ny, 2, 2, 4, 16 * ny).transpose(0, 1, 3, 2, 4)
    my = np.einsum("iplhk,of->iplhokf", y_cells, np.eye(16))
    size_y = 16 * ny * 16
    mz = mz.reshape(nz * 128, nz * 128)
    my = my.reshape(size_y, size_y)

    def wave_term(waves, period):
        return 4.0 / (spacing * spacing) * np.sin(np.pi * waves / period) ** 2

    total = (
        wave_term(wx, 16 * nx)[:, None, None, None]
        + wave_term(wy, 16 * ny)[None, None, :, None]
        + wave_term(wz, 16 * nz).reshape(1, nz, 1, 16)
    )
    return qx, mz, my, total


def split_value(value):
    high = value.astype(jnp.bfloat16)
    low = (value - high.astype(jnp.float32)).astype(jnp.bfloat16)
    return high, low


def product(value, high_ref, low_ref, rows=None):
    high, low = split_value(value)
    if rows is None:
        dims = (((1,), (0,)), ((), ()))
        th, tl = high_ref[...], low_ref[...]
    else:
        dims = (((1,), (1,)), ((), ()))
        th, tl = high_ref[rows, :], low_ref[rows, :]
    dot = functools.partial(
        lax.dot_general, dimension_numbers=dims, preferred_element_type=jnp.float32
    )
    return dot(high, th) + (dot(low, th) + dot(high, tl))


def left_product(high, low, value):
    value_high, value_low = split_value(value)
    dot = functools.partial(jnp.dot, preferred_element_type=jnp.float32)
    return dot(high, value_high) + (dot(high, value_low) + dot(low, value_high))


def exchange_correlation(density):
    positive = density > 0.0
    cube_root = jnp.where(
        positive, jnp.exp(jnp.log(jnp.where(positive, density, 1.0)) * (1.0 / 3.0)), 0.0
    )
    slater = -((3.0 / math.pi) ** (1.0 / 3.0)) * cube_root
    radius = (3.0 / (4.0 * math.pi)) ** (1.0 / 3.0)
    bottom = radius + 7.8 * cube_root
    wigner = -0.44 * cube_root / bottom * (1.0 + radius / (3.0 * bottom))
    return slater + wigner


def window_rows(ref_rows, count):
    return jnp.concatenate([ref_rows(16 * count - 8, 8), ref_rows(0, 24)], axis=0)


def poisson_kernel(counts, all_ref, halo_ref, xh_ref, xl_ref, bh_ref, bl_ref, zh_ref, zl_ref,
                   yh_ref, yl_ref, wave_x, wave_yz, density_ref, potential_ref, modes, back):
    nx, ny, nz = counts
    needed_z = sorted({nz - 1, 0, 1 % nz})
    needed_y = sorted({ny - 1, 0, 1 % ny})

    def run(count, body):
        if count <= 8:
            for index in range(count):
                body(index)
        else:

            def looped(index, carry):
                body(index)
                return carry

            lax.fori_loop(0, count, looped, 0)

    def forward_z(index):
        iy, part = index // 2, index % 2
        value = jnp.concatenate([all_ref[iy, part, iz] for iz in range(nz)], axis=1)
        value = product(value, zh_ref, zl_ref)
        for tile in range(nz):
            modes[tile, index] = value[:, 128 * tile : 128 * tile + 128]

    run(2 * ny, forward_z)

    def middle(tile):
        value = jnp.concatenate([modes[tile, index] for index in range(2 * ny)], axis=1)
        value = product(value, yh_ref, yl_ref)
        value = left_product(xh_ref[...], xl_ref[...], value)
        total = wave_x[...] + wave_yz[tile]
        positive = total > 0.0
        green = jnp.where(positive, 4.0 * math.pi / jnp.where(positive, total, 1.0), 0.0)
        value = left_product(bh_ref[...], bl_ref[...], value * green)
        for iy in needed_y:
            out = product(value, yh_ref, yl_ref, pl.ds(256 * iy, 256))
            for part in range(2):
                back[iy, part, tile] = out[:, 128 * part : 128 * part + 128]

    run(nz, middle)

    for iy in needed_y:
        for part in range(2):
            value = jnp.concatenate([back[iy, part, tile] for tile in range(nz)], axis=1)
            fields = {}
            for iz in needed_z:
                hartree = product(value, zh_ref, zl_ref, pl.ds(128 * iz, 128))
                density = window_rows(
                    lambda start, size: all_ref[iy, part, iz, start : start + size, :], nx
                )
                fields[iz] = hartree + exchange_correlation(density)
            below, own, above = (fields[d % nz] for d in (-1, 0, 1))
            for half in range(2):
                field = joined(below, own, above, half)
                local = 2 * part + half
                targets = []
                if iy == 0:
                    targets.append(2 + local)
                if iy == (ny - 1) and local >= 2:
                    targets.append(local - 2)
                if iy == 1 % ny and local < 2:
                    targets.append(6 + local)
                for chunk in targets:
                    ion = joined(*[halo_ref[d, 1, chunk // 2] for d in range(3)], half)
                    potential_ref[:, 128 * chunk : 128 * chunk + 128] = ion + field
    for part in range(2):
        merged = all_ref[0, part, 0, 0:16, :]
        for half in range(2):
            for inner in range(4):
                b = 8 * part + 4 * half + inner
                shift = (-(32 * inner + 16 * half)) % 128
                piece = pltpu.roll(merged, shift, 1) if shift else merged
                density_ref[:, b, :] = piece[:, 0:16]


def poisson(everything, windows, counts):
    nx, ny, nz = counts
    qx, mz, my, total = tables(counts)
    window = (np.arange(32) - 8) % (16 * nx)
    wave_x = np.broadcast_to(total[:, 0, 0, 0][:, None], (16 * nx, 128)).astype(np.float32)
    wave_x = np.ascontiguousarray(wave_x[:, :1])
    wave_yz = (total[0] - total[0, 0, 0, 0]).reshape(nz, 1, 16 * ny * 16).astype(np.float32)
    constants = (
        *numpy_halves(qx.T),
        *numpy_halves(qx[window]),
        *numpy_halves(mz),
        *numpy_halves(my),
        wave_x,
        wave_yz,
    )
    vmem = pl.BlockSpec(memory_space=pltpu.VMEM)
    return pl.pallas_call(
        functools.partial(poisson_kernel, counts),
        out_shape=(
            jax.ShapeDtypeStruct((16, 16, 16), jnp.float32),
            jax.ShapeDtypeStruct((32, 1024), jnp.float32),
        ),
        in_specs=[vmem] * (2 + len(constants)),
        out_specs=(vmem, vmem),
        scratch_shapes=[
            pltpu.VMEM((nz, 2 * ny, 16 * nx, 128), jnp.float32),
            pltpu.VMEM((ny, 2, nz, 32, 128), jnp.float32),
        ],
        compiler_params=pltpu.CompilerParams(vmem_limit_bytes=63 * 1024 * 1024),
        name="poisson",
    )(everything, windows, *[jnp.asarray(c) for c in constants])


def on_device(counts, orbitals, potential, ion_potential, occupations):
    windows = halo(potential, ion_potential, counts)
    new_orbitals, part = filter_orbitals(occupations, orbitals, windows)
    everything = gather_density(part, counts)
    density, new_potential = poisson(everything, windows, counts)
    return (new_orbitals, density, new_potential)


def solution(mesh):
    counts = (mesh.shape["gx"], mesh.shape["gy"], mesh.shape["gz"])
    placed = (P(None, "gx", ("gy", "gz")), P("gx", "gy", "gz"), P("gx", "gy", "gz"), P())
    return jax.shard_map(
        functools.partial(on_device, counts),
        mesh=mesh,
        in_specs=placed,
        out_specs=(P(None, "gx", ("gy", "gz")), P("gx", "gy", "gz"), P("gx", ("gy", "gz"))),
        check_vma=False,
    )
```
